1024 devices in a mesh: ctx: 8 (over y), exp: 64 (over z, x), rep: 2 (over core).
Axes of the slice: x: 4, y: 8, z: 16, core: 2. Of those that a mesh axis runs over, the one named last changes fastest.
Arguments:
- tokens: bfloat16 [16384, 7168], P(('rep', 'exp'), 'ctx'), parts along dimension 0, may hold values from -6 to 6
- routes: int32 [16384, 2], P(('rep', 'exp')), parts along dimension 0, may hold values from 0 to 63, all different within a row; in each aligned block of 128 rows (0 to 127, 128 to 255, ...) at most 5 rows name the same one
- event_weights: float32 [16384, 2], P(('rep', 'exp')), parts along dimension 0, may hold values from 0.25 to 2
- cotangent: bfloat16 [8192, 7168], P('exp', 'ctx'), may hold values from -0.59765625 to 0.59765625
- w_gate: bfloat16 [64, 7168, 1024], P('exp', 'ctx'), may hold values from -0.0625 to 0.0625
- w_up: bfloat16 [64, 7168, 1024], P('exp', 'ctx'), may hold values from -0.0625 to 0.0625
- w_down: bfloat16 [64, 1024, 7168], P('exp', None, 'ctx'), may hold values from -0.1875 to 0.1875
Outputs:
- mixed: bfloat16 [16384, 7168], P(('rep', 'exp'), 'ctx'), parts along dimension 0
- token_grad: bfloat16 [16384, 7168], P(('rep', 'exp'), 'ctx'), parts along dimension 0
- weight_grad: float32 [16384, 2], P(('rep', 'exp')), parts along dimension 0
The draws below stay inside these ranges and needn't reach their ends.
There are 2 independent parts, one for each index of `rep`. The reference program is written for one: setup_inputs(seed, part) draws one part's arguments, and reference() takes and returns one part's arrays. A program takes and returns all parts, laid end to end along the dimension named above; an argument that names none is the same for every part. Nothing has to cross between parts.
Inputs may be any that keep to these rules, and one draw needn't show every extreme that they name: `routes`: each token names 2 different experts. Among the 128 tokens of one index of exp (aligned blocks of 128 rows) no expert is named more than 5 times, a bound that some block reaches; every expert is named somewhere.
All inputs are finite; a program needn't handle non-finite values.
Results may differ from the reference program's by a relative error of at most 0.03.
Values may be sent and summed in bfloat16 or wider, within the bound.
No kernel may reach another device: no remote copies, remote signals or barrier semaphores. Data moves between devices by JAX's collectives and lax.ppermute only.
A program may use at most 32 MiB of HBM per device.

```python
import math
import jax
import jax.numpy as jnp
import numpy as np
from jax import lax

D = 7168
TOP = 2
FH = 1024
TOK_E = 128
EXPERTS = 64
CAP = 5
TOKENS = 8192
N_CTX = 8
N_EXP = 64


def level_of(rng, dims, shards, low, largest):
    gain, own = 1.0, jax.random.fold_in(rng, 6)
    for position, shards_of in shards:
        draws = jnp.exp(jax.random.uniform(jax.random.fold_in(own, position), (shards_of,), jnp.float32, low / len(shards), largest / len(shards)))
        gain = gain * jnp.repeat(draws, dims[position] // shards_of).reshape([-1 if axis == position else 1 for axis in range(len(dims))])
    return gain


def deal_out(key, own, number, rows, number_of, top, bound, lean):
    sequence = jax.random.permutation(key, number_of)
    crowded, common = portions_of(number_of, rows * top, bound, lean, True), portions_of(number_of, rows * top, bound, lean, False)
    places = jnp.arange(number_of)

    def named(lengths, rotation):
        used = int((lengths > 0).sum())
        fixed = max(1, used // 4)
        passed = fixed + (places - fixed + rotation * (used - fixed)) % max(1, number_of - fixed)
        return jnp.zeros((number_of,), jnp.int32).at[sequence[jnp.where(places < fixed, places, passed)]].set(jnp.asarray(lengths, jnp.int32))

    lengths = jnp.where(number % 4 == 0, named(crowded, number // 4), named(common, number - number // 4 - 1))
    mixed = jax.random.permutation(jax.random.fold_in(own, 3), number_of)
    donor, taker = mixed[0:number_of // 2 * 2:2], mixed[1:number_of // 2 * 2:2]
    slack = jnp.minimum(lengths[donor] - 1, bound - lengths[taker]) // 2
    slack = jnp.where((donor == sequence[0]) | (taker == sequence[0]) | (lengths[taker] == 0), 0, jnp.maximum(slack, 0))
    passed = jax.random.randint(jax.random.fold_in(own, 4), (number_of // 2,), 0, 1 << 20) % (slack + 1)
    lengths = lengths.at[donor].add(-passed).at[taker].add(passed)
    items = jnp.searchsorted(jnp.cumsum(lengths), jnp.arange(rows * top), side="right").astype(jnp.int32)
    table = items.reshape(top, rows).T
    table = table[jax.random.permutation(jax.random.fold_in(own, 1), rows)]
    rotation = jax.random.randint(jax.random.fold_in(own, 2), (rows, 1), 0, top)
    return jnp.take_along_axis(table, (jnp.arange(top)[None, :] + rotation) % top, axis=1)


def portions_of(count, total, most, skew, full):
    loads = [(1 << 20) // math.isqrt(grade ** skew) + 1 for grade in range(1, count + 1)]
    largest = most if full else min(most, max(-(-total // count), total * loads[0] // sum(loads)))
    least = 1 if total - largest >= count - 1 else 0
    given, spare = [largest] + [least] * (count - 1), total - largest - least * (count - 1)
    while spare > 0:
        candidates = [i for i in range(1, count) if given[i] < largest] or [i for i in range(1, count) if given[i] < most]
        mass, remaining = sum([loads[i] for i in candidates]), spare
        for i in candidates:
            extra = min(most - given[i], max(1, remaining * loads[i] // mass), spare)
            given[i] = given[i] + extra
            spare = spare - extra
    return np.array(given)


def bell_draw(own_key, extent, scale, reach, pieces=(), kind=jnp.bfloat16):
    values = scale * jax.random.normal(own_key, extent, jnp.float32)
    if pieces:
        values = values * level_of(own_key, extent, pieces, -0.22, 0.18)
    return jnp.clip(values, -reach, reach).astype(kind)


def setup_inputs(seed: int = 0, part: int = 0) -> dict:
    splits = jax.random.split(jax.random.key(seed), 8)
    own_keys = jax.random.split(jax.random.fold_in(splits[7], part), 8)
    tokens = bell_draw(own_keys[0], (TOKENS, D), 1.0, 6.0, ((0, 64), (1, 8)))
    routes_keys = jax.random.split(jax.random.fold_in(own_keys[1], 1), TOKENS // TOK_E)
    routes_turns = jax.random.permutation(jax.random.fold_in(own_keys[1], 3), TOKENS // TOK_E)
    routes = jax.vmap(lambda own, number: deal_out(jax.random.fold_in(own_keys[1], 2), own, number, TOK_E, EXPERTS, TOP, CAP, 2))(routes_keys, routes_turns).reshape((TOKENS, TOP))
    event_weights = jnp.clip(jnp.exp(math.log(2.0) - 2.0794415 * jax.random.uniform(own_keys[2], (TOKENS, TOP), jnp.float32) ** level_of(own_keys[2], (TOKENS, TOP), ((0, 64),), -0.2, 0.2)), 0.25, 2.0)
    cotangent = bell_draw(splits[3], (TOKENS, D), 0.1, 0.59765625, ((0, 64), (1, 8)))
    w_gate = bell_draw(splits[4], (EXPERTS, D, FH), D ** -0.5, 0.0625, ((0, 64), (1, 8)))
    w_up = bell_draw(splits[5], (EXPERTS, D, FH), D ** -0.5, 0.0625, ((0, 64), (1, 8)))
    w_down = bell_draw(splits[6], (EXPERTS, FH, D), FH ** -0.5, 0.1875, ((0, 64), (2, 8)))
    return dict(tokens=tokens, routes=routes, event_weights=event_weights, cotangent=cotangent, w_gate=w_gate, w_up=w_up, w_down=w_down)


def slot_places(routes):
    routes_flat = routes.reshape(N_EXP, TOK_E * TOP)
    onehot = (routes_flat[:, :, None] == jnp.arange(EXPERTS, dtype=jnp.int32)[None, None, :]).astype(jnp.int32)
    places = jnp.sum((jnp.cumsum(onehot, axis=1) - onehot) * onehot, axis=2)
    source = jnp.arange(N_EXP, dtype=jnp.int32)[:, None]
    return routes_flat.reshape(-1), (source * CAP + places).reshape(-1).astype(jnp.int32)


def rounded_sum(partial_value):
    narrow = lax.optimization_barrier(partial_value.astype(jnp.bfloat16))
    return jnp.sum(narrow.astype(jnp.float32), axis=0)


def activate(gate_pre, up_pre, back_pre):
    squash = jax.nn.sigmoid(gate_pre)
    hidden_act = (gate_pre * squash * up_pre).astype(jnp.bfloat16)
    grad_gate = (back_pre * up_pre * squash * (1.0 + gate_pre * (1.0 - squash))).astype(jnp.bfloat16)
    grad_up = (back_pre * gate_pre * squash).astype(jnp.bfloat16)
    return hidden_act, grad_gate, grad_up


def reference(tokens, routes, event_weights, cotangent, w_gate, w_up, w_down):
    columns = D // N_CTX
    slot_count = N_EXP * CAP
    expert_ids, slot_rows = slot_places(routes)
    token_rows = jnp.repeat(tokens, TOP, axis=0)
    cot_rows = (event_weights.reshape(-1, 1) * jnp.repeat(cotangent.astype(jnp.float32), TOP, axis=0)).astype(jnp.bfloat16)
    token_buffer = jnp.zeros((EXPERTS, slot_count, D), jnp.bfloat16).at[expert_ids, slot_rows].set(token_rows)
    cot_buffer = jnp.zeros((EXPERTS, slot_count, D), jnp.bfloat16).at[expert_ids, slot_rows].set(cot_rows)

    def one_expert(inputs):
        expert_in, expert_cot, gate_mat, up_mat, down_mat = inputs
        blocks_in = expert_in.astype(jnp.float32).reshape(slot_count, N_CTX, columns)
        blocks_cot = expert_cot.astype(jnp.float32).reshape(slot_count, N_CTX, columns)
        gate_blocks = gate_mat.astype(jnp.float32).reshape(N_CTX, columns, FH)
        up_blocks = up_mat.astype(jnp.float32).reshape(N_CTX, columns, FH)
        down_blocks = down_mat.astype(jnp.float32).reshape(FH, N_CTX, columns)
        gate_pre = rounded_sum(jnp.einsum('scd,cdf->csf', blocks_in, gate_blocks))
        up_pre = rounded_sum(jnp.einsum('scd,cdf->csf', blocks_in, up_blocks))
        back_pre = rounded_sum(jnp.einsum('scd,fcd->csf', blocks_cot, down_blocks))
        hidden_act, grad_gate, grad_up = activate(gate_pre, up_pre, back_pre)
        expert_out = jnp.dot(hidden_act, down_mat, preferred_element_type=jnp.float32).astype(jnp.bfloat16)
        event_grad = (jnp.dot(grad_gate, gate_mat.T, preferred_element_type=jnp.float32)
                      + jnp.dot(grad_up, up_mat.T, preferred_element_type=jnp.float32)).astype(jnp.bfloat16)
        return expert_out, event_grad

    out_buffer, grad_buffer = lax.map(one_expert, (token_buffer, cot_buffer, w_gate, w_up, w_down))
    expert_out = out_buffer[expert_ids, slot_rows].reshape(TOKENS, TOP, D).astype(jnp.float32)
    event_grad = grad_buffer[expert_ids, slot_rows].reshape(TOKENS, TOP, D).astype(jnp.float32)
    mixed = jnp.sum(event_weights[:, :, None] * expert_out, axis=1).astype(jnp.bfloat16)
    token_grad = jnp.sum(event_grad, axis=1).astype(jnp.bfloat16)
    weight_grad = jnp.einsum('td,tkd->tk', cotangent.astype(jnp.float32), expert_out)
    return mixed, token_grad, weight_grad
```

```python
import jax
import jax.numpy as jnp
from jax import lax
from jax.sharding import PartitionSpec as P

LANES = 128
F32 = jnp.float32
BF16 = jnp.bfloat16


def matmul(a, b):
    return jnp.dot(a, b, preferred_element_type=F32)


def shards(tokens, routes, event_weights, cotangent, w_gate, w_up, w_down):
    owners = lax.axis_size("exp")
    parts = lax.axis_size("ctx")
    rows, fanout = routes.shape
    _, columns, hidden = w_gate.shape
    capacity = max(2, 5 * rows * fanout // (4 * owners))
    slots = owners * capacity
    piece = hidden // parts
    tiles = capacity * columns // LANES

    flat = routes.reshape(-1)
    named = (flat[:, None] == jnp.arange(owners, dtype=jnp.int32)[None, :]).astype(BF16)
    events = rows * fanout
    earlier = (
        jnp.arange(events)[:, None] > jnp.arange(events)[None, :]
    ).astype(BF16)
    before = matmul(earlier, named)
    places = jnp.sum(before * named.astype(F32), axis=1).astype(jnp.int32)
    targets = (flat * capacity + places).reshape(rows, fanout)
    slot_ids = jnp.arange(slots, dtype=jnp.int32)
    picks = [slot_ids[:, None] == targets[:, k][None, :] for k in range(fanout)]
    pick_any = sum(p.astype(BF16) for p in picks)
    slot_weights = sum(
        jnp.sum(jnp.where(p, event_weights[:, k][None, :], 0.0), axis=1)
        for k, p in enumerate(picks)
    )

    def send(buffer):
        return lax.all_to_all(buffer, "exp", split_axis=0, concat_axis=0, tiled=True)

    send_tokens = matmul(pick_any, tokens).astype(BF16).reshape(owners, tiles, LANES)
    expert_in = send(send_tokens).reshape(slots, columns)
    send_cots = (
        (slot_weights[:, None] * matmul(pick_any, cotangent)).astype(BF16).reshape(owners, tiles, LANES)
    )
    expert_in, send_cots = lax.optimization_barrier((expert_in, send_cots))
    expert_cot = send(send_cots).reshape(slots, columns)

    gate_w = w_gate[0].reshape(columns, parts, piece)
    up_w = w_up[0].reshape(columns, parts, piece)
    down_w = w_down[0].reshape(parts, piece, columns)

    def scatter(value):
        return lax.psum_scatter(value, "ctx", scatter_dimension=0, tiled=False)

    gate_up = jnp.concatenate(
        [
            jnp.einsum("sd,dyj->ysj", expert_in, gate_w, preferred_element_type=F32).astype(BF16),
            jnp.einsum("sd,dyj->ysj", expert_in, up_w, preferred_element_type=F32).astype(BF16),
        ],
        axis=1,
    )
    gate_up = scatter(gate_up).astype(F32)
    gate_pre, up_pre = gate_up[:slots], gate_up[slots:]
    back = jnp.einsum("sd,yjd->ysj", expert_cot, down_w, preferred_element_type=F32).astype(BF16)

    squash = jax.nn.sigmoid(gate_pre)
    hidden_act = (gate_pre * squash * up_pre).astype(BF16)
    hidden_all = lax.all_gather(hidden_act, "ctx", axis=0, tiled=False)
    expert_out = jnp.einsum("ysj,yjd->sd", hidden_all, down_w, preferred_element_type=F32).astype(BF16)
    back_out = send(expert_out.reshape(owners, tiles, LANES)).reshape(slots, columns)

    back_pre = scatter(back).astype(F32)
    grad_gate = (back_pre * up_pre * squash * (1.0 + gate_pre * (1.0 - squash))).astype(BF16)
    grad_up = (back_pre * gate_pre * squash).astype(BF16)
    inner = jnp.sum(hidden_act.astype(F32) * back_pre, axis=1)
    high = lax.reduce_precision(inner, 8, 7)
    inner_rows = jnp.stack([high, inner - high], axis=1).astype(BF16)
    inner_rows = jnp.pad(inner_rows.reshape(-1), (0, 8 * LANES - 2 * slots)).reshape(8, LANES)
    grads = jnp.concatenate([grad_gate, grad_up, inner_rows], axis=0)
    grads = lax.all_gather(grads, "ctx", axis=0, tiled=False)
    inner = jnp.sum(
        grads[:, 2 * slots :, :].reshape(parts, -1)[:, : 2 * slots].reshape(parts, slots, 2).astype(F32),
        axis=(0, 2),
    )
    event_grad = (
        jnp.einsum("ysj,dyj->sd", grads[:, :slots], gate_w, preferred_element_type=F32)
        + jnp.einsum("ysj,dyj->sd", grads[:, slots : 2 * slots], up_w, preferred_element_type=F32)
    ).astype(BF16)
    high = lax.reduce_precision(inner, 8, 7)
    extra = jnp.stack([high, inner - high], axis=1).astype(BF16).reshape(owners, 2 * capacity)
    extra = jnp.pad(extra, ((0, 0), (0, LANES - 2 * capacity)))[:, None, :]
    back_grad = send(jnp.concatenate([event_grad.reshape(owners, tiles, LANES), extra], axis=1))
    inner = jnp.sum(
        back_grad[:, tiles, : 2 * capacity].reshape(slots, 2).astype(F32), axis=1
    )
    back_grad = back_grad[:, :tiles].reshape(slots, columns)

    mixed = sum(
        event_weights[:, k][:, None] * matmul(p.astype(BF16).T, back_out) for k, p in enumerate(picks)
    ).astype(BF16)
    token_grad = matmul(pick_any.T, back_grad).astype(BF16)
    weight_grad = (
        jnp.stack([jnp.sum(jnp.where(p, inner[:, None], 0.0), axis=0) for p in picks], axis=1)
        / event_weights
    )
    return (mixed, token_grad, weight_grad)


def solution(mesh):
    in_specs = (
        P(("rep", "exp"), "ctx"),
        P(("rep", "exp"), None),
        P(("rep", "exp"), None),
        P("exp", "ctx"),
        P("exp", "ctx", None),
        P("exp", "ctx", None),
        P("exp", None, "ctx"),
    )
    out_specs = (P(("rep", "exp"), "ctx"), P(("rep", "exp"), "ctx"), P(("rep", "exp"), None))
    return jax.shard_map(shards, mesh=mesh, in_specs=in_specs, out_specs=out_specs, check_vma=False)
```

```python
import jax
import jax.numpy as jnp
from jax import lax
from jax.sharding import PartitionSpec as P


LANES = 128
F32 = jnp.float32
BF16 = jnp.bfloat16


def matmul(a, b):
    return jnp.dot(a, b, preferred_element_type=F32)


def experts(tokens, routes, event_weights, cotangent, w_gate, w_up, w_down):
    owners = lax.axis_size("exp")
    parts = lax.axis_size("ctx")
    rows, fanout = routes.shape
    _, columns, hidden = w_gate.shape
    capacity = max(2, 5 * rows * fanout // (4 * owners))
    slots = owners * capacity
    piece = hidden // parts
    tiles = capacity * columns // LANES

    flat = routes.reshape(-1)
    named = (flat[:, None] == jnp.arange(owners, dtype=jnp.int32)[None, :]).astype(BF16)
    events = rows * fanout
    earlier = (
        jnp.arange(events)[:, None] > jnp.arange(events)[None, :]
    ).astype(BF16)
    before = matmul(earlier, named)
    places = jnp.sum(before * named.astype(F32), axis=1).astype(jnp.int32)
    targets = (flat * capacity + places).reshape(rows, fanout)
    slot_ids = jnp.arange(slots, dtype=jnp.int32)
    picks = [slot_ids[:, None] == targets[:, k][None, :] for k in range(fanout)]
    pick_any = sum(p.astype(BF16) for p in picks)
    slot_weights = sum(
        jnp.sum(jnp.where(p, event_weights[:, k][None, :], 0.0), axis=1)
        for k, p in enumerate(picks)
    )

    me = lax.axis_index("ctx")

    def send(buffer):
        return lax.all_to_all(buffer, "exp", split_axis=0, concat_axis=0, tiled=True)

    def block(value, step):
        return lax.squeeze(lax.dynamic_slice_in_dim(value, lax.rem(me + step, parts), 1, 0), (0,))

    def shifted(value, step):
        return lax.ppermute(value, "ctx", [(i, (i + step) % parts) for i in range(parts)])

    steps = sorted(range(1, parts), key=lambda step: (min(step, parts - step), step))

    send_tokens = matmul(pick_any, tokens).astype(BF16).reshape(owners, tiles, LANES)
    recv_tokens = send(send_tokens)
    send_cots = (
        (slot_weights[:, None] * matmul(pick_any, cotangent)).astype(BF16).reshape(owners, tiles, LANES)
    )
    gate_w = w_gate[0].reshape(columns, parts, piece).transpose(1, 0, 2)
    up_w = w_up[0].reshape(columns, parts, piece).transpose(1, 0, 2)
    recv_tokens, send_cots, gate_w, up_w = lax.optimization_barrier(
        (recv_tokens, send_cots, gate_w, up_w)
    )
    recv_cots = send(send_cots)
    expert_in = recv_tokens.reshape(slots, columns)
    expert_cot = recv_cots.reshape(slots, columns)

    down_w = w_down[0].reshape(parts, piece, columns)

    gate_up = jnp.concatenate(
        [
            jnp.einsum("sd,ydj->ysj", expert_in, gate_w, preferred_element_type=F32).astype(BF16),
            jnp.einsum("sd,ydj->ysj", expert_in, up_w, preferred_element_type=F32).astype(BF16),
        ],
        axis=1,
    )
    arrived = [shifted(block(gate_up, step), step) for step in steps]
    gate_up = sum((a.astype(F32) for a in arrived), block(gate_up, 0).astype(F32))
    gate_pre, up_pre = gate_up[:slots], gate_up[slots:]
    squash = jax.nn.sigmoid(gate_pre)
    hidden_act = (gate_pre * squash * up_pre).astype(BF16)

    back = jnp.einsum("sd,yjd->ysj", expert_cot, down_w, preferred_element_type=F32).astype(BF16)
    hidden_act, back = lax.optimization_barrier((hidden_act, back))
    back = lax.all_to_all(back, "ctx", split_axis=0, concat_axis=0, tiled=True)
    hidden_all = lax.all_gather(hidden_act, "ctx", axis=0, tiled=False)
    expert_out = jnp.einsum("ysj,yjd->sd", hidden_all, down_w, preferred_element_type=F32).astype(BF16)
    back, send_out = lax.optimization_barrier((back, expert_out.reshape(owners, tiles, LANES)))
    back_out = send(send_out)

    back_pre = jnp.sum(back.astype(F32), axis=0)
    grad_gate = (back_pre * up_pre * squash * (1.0 + gate_pre * (1.0 - squash))).astype(BF16)
    grad_up = (back_pre * gate_pre * squash).astype(BF16)
    inner = jnp.sum(hidden_act.astype(F32) * back_pre, axis=1)
    high = lax.reduce_precision(inner, 8, 7)
    inner_rows = jnp.stack([high, inner - high], axis=0).astype(BF16)
    inner_rows = jnp.pad(inner_rows.reshape(-1), (0, 8 * LANES - 2 * slots)).reshape(8, LANES)
    grads = jnp.concatenate([grad_gate, grad_up, inner_rows], axis=0)
    arrived = [shifted(grads, -step) for step in steps]
    gathered = jnp.zeros((parts, *grads.shape), BF16)
    for step, value in zip([0, *steps], [grads, *arrived]):
        gathered = lax.dynamic_update_slice(gathered, value[None], (lax.rem(me + step, parts), 0, 0))
    grads = gathered
    inner = jnp.sum(grads[:, 2 * slots :, :].reshape(parts, -1).astype(F32), axis=0)
    inner = inner[:slots] + inner[slots : 2 * slots]
    event_grad = (
        jnp.einsum("ysj,ydj->sd", grads[:, :slots], gate_w, preferred_element_type=F32)
        + jnp.einsum("ysj,ydj->sd", grads[:, slots : 2 * slots], up_w, preferred_element_type=F32)
    ).astype(BF16)
    high = lax.reduce_precision(inner, 8, 7)
    extra = jnp.concatenate(
        [high.reshape(owners, capacity), (inner - high).reshape(owners, capacity)], axis=1
    ).astype(BF16)
    extra = jnp.pad(extra, ((0, 0), (0, LANES - 2 * capacity)))[:, None, :]
    back_grad = send(jnp.concatenate([event_grad.reshape(owners, tiles, LANES), extra], axis=1))
    back_out = back_out.reshape(slots, columns)
    extra = back_grad[:, tiles, : 2 * capacity].astype(F32)
    inner = (extra[:, :capacity] + extra[:, capacity:]).reshape(slots)
    back_grad = back_grad[:, :tiles].reshape(slots, columns)

    mixed = sum(
        event_weights[:, k][:, None] * matmul(p.astype(BF16).T, back_out) for k, p in enumerate(picks)
    ).astype(BF16)
    token_grad = matmul(pick_any.T, back_grad).astype(BF16)
    weight_grad = (
        jnp.stack([jnp.sum(jnp.where(p, inner[:, None], 0.0), axis=0) for p in picks], axis=1)
        / event_weights
    )
    return (mixed, token_grad, weight_grad)


def solution(mesh):
    in_specs = (
        P(("rep", "exp"), "ctx"),
        P(("rep", "exp"), None),
        P(("rep", "exp"), None),
        P("exp", "ctx"),
        P("exp", "ctx", None),
        P("exp", "ctx", None),
        P("exp", None, "ctx"),
    )
    out_specs = (P(("rep", "exp"), "ctx"), P(("rep", "exp"), "ctx"), P(("rep", "exp"), None))
    return jax.shard_map(experts, mesh=mesh, in_specs=in_specs, out_specs=out_specs, check_vma=False)
```

```python
import jax
import jax.numpy as jnp
from jax import lax
from jax.sharding import Mesh
from jax.sharding import PartitionSpec as P


LANES = 128
ALONG_X = 4
F32 = jnp.float32
BF16 = jnp.bfloat16


def matmul(a, b):
    return jnp.dot(a, b, preferred_element_type=F32)


def experts(tokens, routes, event_weights, cotangent, w_gate, w_up, w_down):
    along_z, along_x = lax.axis_size("z"), lax.axis_size("x")
    owners = along_z * along_x
    parts = lax.axis_size("ctx")
    rows, fanout = routes.shape
    _, columns, hidden = w_gate.shape
    capacity = max(2, 5 * rows * fanout // (4 * owners))
    slots = owners * capacity
    piece = hidden // parts
    column = along_z * capacity
    tiles = along_x * capacity * columns // LANES

    flat = routes.reshape(-1)
    named = (flat[:, None] == jnp.arange(owners, dtype=jnp.int32)[None, :]).astype(BF16)
    events = rows * fanout
    earlier = (
        jnp.arange(events)[:, None] > jnp.arange(events)[None, :]
    ).astype(BF16)
    before = matmul(earlier, named)
    places = jnp.sum(before * named.astype(F32), axis=1).astype(jnp.int32)
    steps_x = lax.rem(lax.rem(flat, along_x) - lax.axis_index("x") + along_x, along_x)
    targets = (steps_x * column + flat // along_x * capacity + places).reshape(rows, fanout)
    from_z = (flat // along_x).reshape(rows, fanout)
    from_lane = (steps_x * capacity + places).reshape(rows, fanout)
    slot_ids = jnp.arange(slots, dtype=jnp.int32)
    picks = [slot_ids[:, None] == targets[:, k][None, :] for k in range(fanout)]
    pick_any = sum(p.astype(BF16) for p in picks)
    slot_weights = sum(
        jnp.sum(jnp.where(p, event_weights[:, k][None, :], 0.0), axis=1)
        for k, p in enumerate(picks)
    )

    me = lax.axis_index("ctx")

    def along(value, step):
        return lax.ppermute(value, "x", [(i, (i + step) % along_x) for i in range(along_x)])

    def exchange(buffer):
        return lax.all_to_all(buffer, "z", split_axis=0, concat_axis=0, tiled=True)

    by_z = jnp.arange(slots, dtype=jnp.int32)
    wide = along_x * capacity
    by_z = by_z % wide // capacity * column + by_z // wide * capacity + by_z % capacity
    reorder = (by_z[:, None] == slot_ids[None, :]).astype(BF16)

    def to_columns(value):
        pieces = [value[step * column : (step + 1) * column] for step in range(along_x)]
        pieces = [pieces[0]] + [along(pieces[step], step) for step in range(1, along_x)]
        pieces = matmul(reorder, jnp.concatenate(pieces, axis=0)).astype(BF16)
        return pieces.reshape(along_z, tiles, LANES)

    def from_columns(value, tail=None):
        value = matmul(reorder.T, value.reshape(slots, columns)).astype(BF16)
        pieces = [value[step * column : (step + 1) * column] for step in range(along_x)]
        if tail is not None:
            pieces = [jnp.concatenate([piece, tail], axis=0) for piece in pieces]
        return [pieces[0]] + [along(pieces[step], -step) for step in range(1, along_x)]

    def block(value, step):
        return lax.squeeze(lax.dynamic_slice_in_dim(value, lax.rem(me + step, parts), 1, 0), (0,))

    def shifted(value, step):
        return lax.ppermute(value, "ctx", [(i, (i + step) % parts) for i in range(parts)])

    steps = sorted(range(1, parts), key=lambda step: (min(step, parts - step), step))

    send_tokens = to_columns(matmul(pick_any, tokens).astype(BF16))
    recv_tokens = exchange(send_tokens)
    send_cots = to_columns((slot_weights[:, None] * matmul(pick_any, cotangent)).astype(BF16))
    gate_w = w_gate[0].reshape(columns, parts, piece).transpose(1, 0, 2)
    up_w = w_up[0].reshape(columns, parts, piece).transpose(1, 0, 2)
    recv_tokens, send_cots, gate_w, up_w = lax.optimization_barrier(
        (recv_tokens, send_cots, gate_w, up_w)
    )
    recv_cots = exchange(send_cots)
    expert_in = recv_tokens.reshape(slots, columns)
    expert_cot = recv_cots.reshape(slots, columns)

    down_w = w_down[0].reshape(parts, piece, columns)

    gate_up = jnp.concatenate(
        [
            jnp.einsum("sd,ydj->ysj", expert_in, gate_w, preferred_element_type=F32).astype(BF16),
            jnp.einsum("sd,ydj->ysj", expert_in, up_w, preferred_element_type=F32).astype(BF16),
        ],
        axis=1,
    )
    arrived = [shifted(block(gate_up, step), step) for step in steps]
    gate_up = sum((a.astype(F32) for a in arrived), block(gate_up, 0).astype(F32))
    gate_pre, up_pre = gate_up[:slots], gate_up[slots:]
    squash = jax.nn.sigmoid(gate_pre)
    hidden_act = (gate_pre * squash * up_pre).astype(BF16)

    back = jnp.einsum("sd,yjd->ysj", expert_cot, down_w, preferred_element_type=F32).astype(BF16)
    mixed_rows = jnp.concatenate([back, jnp.broadcast_to(hidden_act, back.shape)], axis=1)
    mixed_rows = lax.all_to_all(mixed_rows, "ctx", split_axis=0, concat_axis=0, tiled=True)
    back, hidden_all = mixed_rows[:, :slots], mixed_rows[:, slots:]
    expert_out = jnp.einsum("ysj,yjd->sd", hidden_all, down_w, preferred_element_type=F32).astype(BF16)
    back_out = exchange(expert_out.reshape(along_z, tiles, LANES))

    back_pre = jnp.sum(back.astype(F32), axis=0)
    grad_gate = (back_pre * up_pre * squash * (1.0 + gate_pre * (1.0 - squash))).astype(BF16)
    grad_up = (back_pre * gate_pre * squash).astype(BF16)
    inner = jnp.sum(hidden_act.astype(F32) * back_pre, axis=1)
    high = lax.reduce_precision(inner, 8, 7)
    inner_rows = jnp.stack([high, inner - high], axis=0).astype(BF16)
    inner_rows = jnp.pad(inner_rows.reshape(-1), (0, 8 * LANES - 2 * slots)).reshape(8, LANES)
    grads = jnp.concatenate([grad_gate, grad_up, inner_rows], axis=0)
    arrived = [shifted(grads, -step) for step in steps]
    gathered = jnp.zeros((parts, *grads.shape), BF16)
    for step, value in zip([0, *steps], [grads, *arrived]):
        gathered = lax.dynamic_update_slice(gathered, value[None], (lax.rem(me + step, parts), 0, 0))
    grads = gathered
    inner = jnp.sum(grads[:, 2 * slots :, :].reshape(parts, -1).astype(F32), axis=0)
    inner = inner[:slots] + inner[slots : 2 * slots]
    event_grad = (
        jnp.einsum("ysj,ydj->sd", grads[:, :slots], gate_w, preferred_element_type=F32)
        + jnp.einsum("ysj,ydj->sd", grads[:, slots : 2 * slots], up_w, preferred_element_type=F32)
    ).astype(BF16)
    high = lax.reduce_precision(inner, 8, 7)
    extra = jnp.concatenate(
        [high.reshape(along_z, -1), (inner - high).reshape(along_z, -1)], axis=1
    ).astype(BF16)
    extra = jnp.pad(extra, ((0, 0), (0, LANES - 2 * wide)))[:, None, :]
    back_grad = exchange(
        jnp.concatenate([event_grad.reshape(along_z, tiles, LANES), extra], axis=1)
    )
    back_out = jnp.concatenate(from_columns(back_out), axis=0)
    tail = jnp.pad(back_grad[:, tiles], ((0, 0), (0, columns - LANES)))
    pieces = from_columns(back_grad[:, :tiles], tail)
    back_grad = jnp.concatenate([piece[:column] for piece in pieces], axis=0)
    lane = jnp.arange(LANES, dtype=jnp.int32)[None, :]
    inner = sum(
        jnp.where(lane % wide // capacity == step, piece[column:, :LANES], 0)
        for step, piece in enumerate(pieces)
    )

    mixed = sum(
        event_weights[:, k][:, None] * matmul(p.astype(BF16).T, back_out) for k, p in enumerate(picks)
    ).astype(BF16)
    token_grad = matmul(pick_any.T, back_grad).astype(BF16)
    z_ids = jnp.arange(along_z, dtype=jnp.int32)[None, :]
    weight_grad = []
    for k in range(fanout):
        values = matmul((from_z[:, k][:, None] == z_ids).astype(BF16), inner)
        held = (lane < 2 * wide) & (lane % wide == from_lane[:, k][:, None])
        weight_grad.append(jnp.sum(jnp.where(held, values, 0.0), axis=1))
    weight_grad = jnp.stack(weight_grad, axis=1) / event_weights
    return (mixed, token_grad, weight_grad)


def solution(mesh):
    parts, owners, reps = mesh.devices.shape
    chips = mesh.devices.reshape(parts, owners // ALONG_X, ALONG_X, reps)
    grid = Mesh(chips, ("ctx", "z", "x", "rep"))
    rows = P(("rep", "z", "x"), "ctx")
    pairs = P(("rep", "z", "x"), None)
    in_specs = (
        rows,
        pairs,
        pairs,
        P(("z", "x"), "ctx"),
        P(("z", "x"), "ctx", None),
        P(("z", "x"), "ctx", None),
        P(("z", "x"), None, "ctx"),
    )
    return jax.shard_map(experts, mesh=grid, in_specs=in_specs, out_specs=(rows, rows, pairs), check_vma=False)
```

```python
import jax
import jax.numpy as jnp
from jax import lax
from jax.sharding import PartitionSpec as P

LANES = 128
F32 = jnp.float32
BF16 = jnp.bfloat16


def matmul(a, b):
    return jnp.dot(a, b, preferred_element_type=F32)


def shards(tokens, routes, event_weights, cotangent, w_gate, w_up, w_down):
    owners = lax.axis_size("exp")
    parts = lax.axis_size("ctx")
    rows, fanout = routes.shape
    _, columns, hidden = w_gate.shape
    capacity = max(2, 5 * rows * fanout // (4 * owners))
    slots = owners * capacity
    piece = hidden // parts
    tiles = capacity * columns // LANES

    flat = routes.reshape(-1)
    named = (flat[:, None] == jnp.arange(owners, dtype=jnp.int32)[None, :]).astype(BF16)
    events = rows * fanout
    earlier = (
        jnp.arange(events)[:, None] > jnp.arange(events)[None, :]
    ).astype(BF16)
    before = matmul(earlier, named)
    places = jnp.sum(before * named.astype(F32), axis=1).astype(jnp.int32)
    targets = (flat * capacity + places).reshape(rows, fanout)
    slot_ids = jnp.arange(slots, dtype=jnp.int32)
    picks = [slot_ids[:, None] == targets[:, k][None, :] for k in range(fanout)]
    pick_any = sum(p.astype(BF16) for p in picks)
    slot_weights = sum(
        jnp.sum(jnp.where(p, event_weights[:, k][None, :], 0.0), axis=1)
        for k, p in enumerate(picks)
    )

    def send(buffer):
        return lax.all_to_all(buffer, "exp", split_axis=0, concat_axis=0, tiled=True)

    with jax.named_scope("send_tokens"):
        send_tokens = matmul(pick_any, tokens).astype(BF16).reshape(owners, tiles, LANES)
        recv_tokens = send(send_tokens)
    send_cots = (
        (slot_weights[:, None] * matmul(pick_any, cotangent)).astype(BF16).reshape(owners, tiles, LANES)
    )
    gate_w = w_gate[0].reshape(columns, parts, piece).transpose(1, 0, 2)
    up_w = w_up[0].reshape(columns, parts, piece).transpose(1, 0, 2)
    recv_tokens, send_cots, gate_w, up_w = lax.optimization_barrier(
        (recv_tokens, send_cots, gate_w, up_w)
    )
    with jax.named_scope("send_cots"):
        recv_cots = send(send_cots)
    expert_in = recv_tokens.reshape(slots, columns)
    expert_cot = recv_cots.reshape(slots, columns)

    down_w = w_down[0].reshape(parts, piece, columns)

    gate_up = jnp.concatenate(
        [
            jnp.einsum("sd,ydj->ysj", expert_in, gate_w, preferred_element_type=F32).astype(BF16),
            jnp.einsum("sd,ydj->ysj", expert_in, up_w, preferred_element_type=F32).astype(BF16),
        ],
        axis=1,
    )
    with jax.named_scope("reduce_gate_up"):
        gate_up = lax.psum_scatter(gate_up, "ctx", scatter_dimension=0, tiled=False).astype(F32)
    gate_pre, up_pre = gate_up[:slots], gate_up[slots:]
    squash = jax.nn.sigmoid(gate_pre)
    hidden_act = (gate_pre * squash * up_pre).astype(BF16)

    with jax.named_scope("back_product"):
        back = jnp.einsum("sd,yjd->ysj", expert_cot, down_w, preferred_element_type=F32).astype(BF16)
    hidden_act, _ = lax.optimization_barrier((hidden_act, back))
    with jax.named_scope("reduce_back"):
        back = lax.all_to_all(back, "ctx", split_axis=0, concat_axis=0, tiled=True)
    with jax.named_scope("gather_hidden"):
        hidden_all = lax.all_gather(hidden_act, "ctx", axis=0, tiled=False)
    expert_out = jnp.einsum("ysj,yjd->sd", hidden_all, down_w, preferred_element_type=F32).astype(BF16)
    back, send_out = lax.optimization_barrier((back, expert_out.reshape(owners, tiles, LANES)))
    with jax.named_scope("send_out"):
        back_out = send(send_out)

    back_pre = jnp.sum(back.astype(F32), axis=0)
    grad_gate = (back_pre * up_pre * squash * (1.0 + gate_pre * (1.0 - squash))).astype(BF16)
    grad_up = (back_pre * gate_pre * squash).astype(BF16)
    inner = jnp.sum(hidden_act.astype(F32) * back_pre, axis=1)
    high = lax.reduce_precision(inner, 8, 7)
    inner_rows = jnp.stack([high, inner - high], axis=0).astype(BF16)
    inner_rows = jnp.pad(inner_rows.reshape(-1), (0, 8 * LANES - 2 * slots)).reshape(8, LANES)
    grads = jnp.concatenate([grad_gate, grad_up, inner_rows], axis=0)
    with jax.named_scope("gather_grads"):
        grads = lax.all_gather(grads, "ctx", axis=0, tiled=False)
    inner = jnp.sum(grads[:, 2 * slots :, :].reshape(parts, -1).astype(F32), axis=0)
    inner = inner[:slots] + inner[slots : 2 * slots]
    event_grad = (
        jnp.einsum("ysj,ydj->sd", grads[:, :slots], gate_w, preferred_element_type=F32)
        + jnp.einsum("ysj,ydj->sd", grads[:, slots : 2 * slots], up_w, preferred_element_type=F32)
    ).astype(BF16)
    high = lax.reduce_precision(inner, 8, 7)
    extra = jnp.concatenate(
        [high.reshape(owners, capacity), (inner - high).reshape(owners, capacity)], axis=1
    ).astype(BF16)
    extra = jnp.pad(extra, ((0, 0), (0, LANES - 2 * capacity)))[:, None, :]
    with jax.named_scope("send_grad"):
        back_grad = send(jnp.concatenate([event_grad.reshape(owners, tiles, LANES), extra], axis=1))
    back_out = back_out.reshape(slots, columns)
    extra = back_grad[:, tiles, : 2 * capacity].astype(F32)
    inner = (extra[:, :capacity] + extra[:, capacity:]).reshape(slots)
    back_grad = back_grad[:, :tiles].reshape(slots, columns)

    mixed = sum(
        event_weights[:, k][:, None] * matmul(p.astype(BF16).T, back_out) for k, p in enumerate(picks)
    ).astype(BF16)
    token_grad = matmul(pick_any.T, back_grad).astype(BF16)
    weight_grad = (
        jnp.stack([jnp.sum(jnp.where(p, inner[:, None], 0.0), axis=0) for p in picks], axis=1)
        / event_weights
    )
    return (mixed, token_grad, weight_grad)


def solution(mesh):
    in_specs = (
        P(("rep", "exp"), "ctx"),
        P(("rep", "exp"), None),
        P(("rep", "exp"), None),
        P("exp", "ctx"),
        P("exp", "ctx", None),
        P("exp", "ctx", None),
        P("exp", None, "ctx"),
    )
    out_specs = (P(("rep", "exp"), "ctx"), P(("rep", "exp"), "ctx"), P(("rep", "exp"), None))
    return jax.shard_map(shards, mesh=mesh, in_specs=in_specs, out_specs=out_specs, check_vma=False)
```

```python
import jax
import jax.numpy as jnp
from jax import lax
from jax.sharding import PartitionSpec as P

LANES = 128
F32 = jnp.float32
BF16 = jnp.bfloat16


def matmul(a, b):
    return jnp.dot(a, b, preferred_element_type=F32)


def shards(tokens, routes, event_weights, cotangent, w_gate, w_up, w_down):
    owners = lax.axis_size("exp")
    parts = lax.axis_size("ctx")
    rows, fanout = routes.shape
    _, columns, hidden = w_gate.shape
    capacity = max(2, 5 * rows * fanout // (4 * owners))
    slots = owners * capacity
    piece = hidden // parts
    tiles = capacity * columns // LANES

    flat = routes.reshape(-1)
    named = (flat[:, None] == jnp.arange(owners, dtype=jnp.int32)[None, :]).astype(BF16)
    events = rows * fanout
    earlier = (
        jnp.arange(events)[:, None] > jnp.arange(events)[None, :]
    ).astype(BF16)
    before = matmul(earlier, named)
    places = jnp.sum(before * named.astype(F32), axis=1).astype(jnp.int32)
    targets = (flat * capacity + places).reshape(rows, fanout)
    slot_ids = jnp.arange(slots, dtype=jnp.int32)
    picks = [slot_ids[:, None] == targets[:, k][None, :] for k in range(fanout)]
    pick_any = sum(p.astype(BF16) for p in picks)
    slot_weights = sum(
        jnp.sum(jnp.where(p, event_weights[:, k][None, :], 0.0), axis=1)
        for k, p in enumerate(picks)
    )

    def send(buffer):
        return lax.all_to_all(buffer, "exp", split_axis=0, concat_axis=0, tiled=True)

    def spread(value):
        return lax.all_to_all(value, "ctx", split_axis=0, concat_axis=0, tiled=True)

    send_tokens = matmul(pick_any, tokens).astype(BF16)
    send_cots = (slot_weights[:, None] * matmul(pick_any, cotangent)).astype(BF16)
    received = send(
        jnp.concatenate(
            [send_tokens.reshape(owners, tiles, LANES), send_cots.reshape(owners, tiles, LANES)], axis=1
        )
    )
    gate_w = w_gate[0].reshape(columns, parts, piece).transpose(1, 0, 2)
    up_w = w_up[0].reshape(columns, parts, piece).transpose(1, 0, 2)
    received, gate_w, up_w = lax.optimization_barrier((received, gate_w, up_w))
    expert_in = received[:, :tiles].reshape(slots, columns)
    expert_cot = received[:, tiles:].reshape(slots, columns)
    down_w = w_down[0].reshape(parts, piece, columns)

    partial = jnp.concatenate(
        [
            jnp.einsum("sd,ydj->ysj", expert_in, gate_w, preferred_element_type=F32).astype(BF16),
            jnp.einsum("sd,ydj->ysj", expert_in, up_w, preferred_element_type=F32).astype(BF16),
            jnp.einsum("sd,yjd->ysj", expert_cot, down_w, preferred_element_type=F32).astype(BF16),
        ],
        axis=1,
    )
    pre = jnp.sum(spread(partial).astype(F32), axis=0)
    gate_pre, up_pre, back_pre = pre[:slots], pre[slots : 2 * slots], pre[2 * slots :]
    squash = jax.nn.sigmoid(gate_pre)
    hidden_act = (gate_pre * squash * up_pre).astype(BF16)
    grad_gate = (back_pre * up_pre * squash * (1.0 + gate_pre * (1.0 - squash))).astype(BF16)
    grad_up = (back_pre * gate_pre * squash).astype(BF16)
    inner = jnp.sum(hidden_act.astype(F32) * back_pre, axis=1)
    high = lax.reduce_precision(inner, 8, 7)
    inner_rows = jnp.stack([high, inner - high], axis=0).astype(BF16)
    inner_rows = jnp.pad(inner_rows.reshape(-1), (0, 8 * LANES - 2 * slots)).reshape(8, LANES)
    own = jnp.concatenate([hidden_act, grad_gate, grad_up, inner_rows], axis=0)
    every = spread(jnp.broadcast_to(own[None], (parts, *own.shape)))
    expert_out = jnp.einsum(
        "ysj,yjd->sd", every[:, :slots], down_w, preferred_element_type=F32
    ).astype(BF16)
    event_grad = (
        jnp.einsum("ysj,ydj->sd", every[:, slots : 2 * slots], gate_w, preferred_element_type=F32)
        + jnp.einsum("ysj,ydj->sd", every[:, 2 * slots : 3 * slots], up_w, preferred_element_type=F32)
    ).astype(BF16)
    inner = jnp.sum(every[:, 3 * slots :, :].reshape(parts, -1).astype(F32), axis=0)
    inner = inner[:slots] + inner[slots : 2 * slots]
    high = lax.reduce_precision(inner, 8, 7)
    extra = jnp.concatenate(
        [high.reshape(owners, capacity), (inner - high).reshape(owners, capacity)], axis=1
    ).astype(BF16)
    extra = jnp.pad(extra, ((0, 0), (0, LANES - 2 * capacity)))[:, None, :]
    returned = send(
        jnp.concatenate(
            [expert_out.reshape(owners, tiles, LANES), event_grad.reshape(owners, tiles, LANES), extra], axis=1
        )
    )
    back_out = returned[:, :tiles].reshape(slots, columns)
    back_grad = returned[:, tiles : 2 * tiles].reshape(slots, columns)
    extra = returned[:, 2 * tiles, : 2 * capacity].astype(F32)
    inner = (extra[:, :capacity] + extra[:, capacity:]).reshape(slots)

    mixed = sum(
        event_weights[:, k][:, None] * matmul(p.astype(BF16).T, back_out) for k, p in enumerate(picks)
    ).astype(BF16)
    token_grad = matmul(pick_any.T, back_grad).astype(BF16)
    weight_grad = (
        jnp.stack([jnp.sum(jnp.where(p, inner[:, None], 0.0), axis=0) for p in picks], axis=1)
        / event_weights
    )
    return (mixed, token_grad, weight_grad)


def solution(mesh):
    in_specs = (
        P(("rep", "exp"), "ctx"),
        P(("rep", "exp"), None),
        P(("rep", "exp"), None),
        P("exp", "ctx"),
        P("exp", "ctx", None),
        P("exp", "ctx", None),
        P("exp", None, "ctx"),
    )
    out_specs = (P(("rep", "exp"), "ctx"), P(("rep", "exp"), "ctx"), P(("rep", "exp"), None))
    return jax.shard_map(shards, mesh=mesh, in_specs=in_specs, out_specs=out_specs, check_vma=False)
```
